32 devices in a mesh: seq: 16 (over z, y, core), dp: 2 (over x).
Axes of the slice: x: 2, y: 2, z: 4, core: 2. Of those that a mesh axis runs over, the one named last changes fastest.
Arguments:
- queries: bfloat16 [2, 4096, 2048], P('dp', 'seq'), may hold values from -6 to 6
- key_rows: bfloat16 [2, 4096, 2048], P('dp', 'seq'), may hold values from -6 to 6
- value_rows: bfloat16 [2, 4096, 2048], P('dp', 'seq'), may hold values from -6 to 6
- out_grad: bfloat16 [2, 4096, 2048], P('dp', 'seq'), may hold values from -6 to 6
- out_weight: bfloat16 [2048, 2048], P('seq', 'dp'), may hold values from -0.125 to 0.125
Outputs:
- query_grad: bfloat16 [2, 4096, 2048], P('dp', 'seq')
- key_grad: bfloat16 [2, 4096, 2048], P('dp', 'seq')
- value_grad: bfloat16 [2, 4096, 2048], P('dp', 'seq')
- weight_grad: float32 [2048, 2048], P('seq', 'dp')
The draws below stay inside these ranges and needn't reach their ends.
All inputs are finite; a program needn't handle non-finite values.
Results may differ from the reference program's by a relative error of at most 0.014.
Values may be sent and summed in bfloat16 or wider, within the bound.
A program may use at most 192 MiB of HBM per device.

```python
import math
import jax
import jax.numpy as jnp
from jax import lax

HEADS = 16
HEAD = 128
DW = 2048
TOK_DEV = 256
HD = 2048
LENGTH = 4096
NSEQ = 2


def raised(values, own_key, source, target, blocks, factor):
    def block_of(position):
        return (jnp.arange(values.shape[position]) // (values.shape[position] // blocks)).reshape((-1,) + (1,) * (values.ndim - 1 - position))

    one_side = jax.random.permutation(own_key, blocks)[block_of(target)]
    second = (block_of(target) + blocks // 2) % blocks
    return jnp.where((block_of(source) == one_side) | (block_of(source) == second), factor * values, values)


def shard_levels(key, shape, pieces, least, largest):
    level = 1.0
    for position, parts in pieces:
        draws = jax.random.uniform(jax.random.fold_in(jax.random.fold_in(key, 6), position), (parts,), jnp.float32, least / len(pieces), largest / len(pieces))
        level = level * jnp.repeat(jnp.exp(draws), shape[position] // parts).reshape((-1,) + (1,) * (len(shape) - 1 - position))
    return level


def centred(rng, extent, scale, most, cuts=(), kind=jnp.bfloat16):
    factor_of = shard_levels(rng, extent, cuts, -0.22, 0.18) if cuts else 1.0
    entries = jax.random.normal(rng, extent, jnp.float32) * scale * factor_of
    return jnp.minimum(jnp.maximum(entries, -most), most).astype(kind)


def noise_with(rng, extent, width, bound, cuts, heavy, kind=jnp.bfloat16):
    drawn = width * jax.random.normal(rng, extent, jnp.float32)
    if cuts:
        drawn = drawn * shard_levels(rng, extent, cuts, -0.22, 0.18)
    return jnp.clip(raised(drawn, jax.random.fold_in(rng, 3), *heavy), -bound, bound).astype(kind)


def setup_inputs(seed: int = 0) -> dict:
    keys = jax.random.split(jax.random.key(seed), 6)
    return {
        "queries": centred(keys[0], (NSEQ, LENGTH, HD), 1.0, 6.0, ((0, 2), (1, 16))),
        "key_rows": centred(keys[1], (NSEQ, LENGTH, HD), 1.0, 6.0, ((0, 2), (1, 16))),
        "value_rows": centred(keys[2], (NSEQ, LENGTH, HD), 1.0, 6.0, ((0, 2), (1, 16))),
        "out_grad": noise_with(keys[3], (NSEQ, LENGTH, DW), 1.0, 6.0, ((0, 2), (1, 16)), (1, 2, 16, 2.0)),
        "out_weight": centred(keys[4], (HD, DW), HD ** -0.5, 0.125, ((0, 16), (1, 2))),
    }


def settle(values_in):
    return lax.optimization_barrier(values_in.astype(jnp.bfloat16)).astype(jnp.float32)

def reference(queries, key_rows, value_rows, out_grad, out_weight):
    seq_count = queries.shape[0]
    seq_length = queries.shape[1]
    blocks = seq_length // TOK_DEV
    score_scale = 1.0 / math.sqrt(HEAD * seq_length)
    grad_scale = 1.0 / math.sqrt(seq_count * seq_length)
    row_ids = jnp.arange(TOK_DEV, dtype=jnp.int32)
    causal = (row_ids[:, None] >= row_ids[None, :]).astype(jnp.float32)

    def split_heads(block_rows):
        return block_rows.reshape(TOK_DEV, HEADS, HEAD).astype(jnp.float32)

    def one_sequence(seq_item):
        query_seq, key_seq, value_seq, grad_seq = seq_item
        query_blocks = query_seq.reshape(blocks, TOK_DEV, HD)
        key_blocks = key_seq.reshape(blocks, TOK_DEV, HD)
        value_blocks = value_seq.reshape(blocks, TOK_DEV, HD)
        grad_blocks = grad_seq.reshape(blocks, TOK_DEV, DW)

        def forward(carry, block_item):
            kv_state, weight_acc = carry
            query_b, key_b, value_b, grad_b = block_item
            query_h = split_heads(query_b)
            key_h = split_heads(key_b)
            value_h = split_heads(value_b)
            prefix_scaled = settle(score_scale * kv_state)
            scores = settle(score_scale * jnp.einsum('thd,shd->hts', query_h, key_h) * causal)
            attended = jnp.einsum('hts,shd->thd', scores, value_h) + jnp.einsum('thd,hde->the', query_h, prefix_scaled)
            attended = attended.astype(jnp.bfloat16).reshape(TOK_DEV, HD)
            head_grad = jnp.dot(grad_b, out_weight.T, preferred_element_type=jnp.float32).astype(jnp.bfloat16)
            weight_acc = weight_acc + grad_scale * jnp.dot(attended.T, grad_b, preferred_element_type=jnp.float32)
            query_dout = jnp.einsum('thd,the->hde', query_h, split_heads(head_grad))
            kv_state = kv_state + jnp.einsum('shd,she->hde', key_h, value_h)
            return ((kv_state, weight_acc), (prefix_scaled, head_grad, query_dout))
        start_state = jnp.zeros((HEADS, HEAD, HEAD), jnp.float32)
        start_weight = jnp.zeros((HD, DW), jnp.float32)
        (_, weight_acc), (prefixes, head_grads, query_douts) = lax.scan(forward, (start_state, start_weight), (query_blocks, key_blocks, value_blocks, grad_blocks))

        def backward(grad_state, local_sum):
            return (grad_state + local_sum, grad_state)
        _, suffixes = lax.scan(backward, start_state, query_douts, reverse=True)

        def gradients(dummy, block_item):
            query_b, key_b, value_b, head_grad, prefix_scaled, suffix = block_item
            query_h = split_heads(query_b)
            key_h = split_heads(key_b)
            value_h = split_heads(value_b)
            grad_h = split_heads(head_grad)
            suffix_scaled = settle(score_scale * suffix)
            scores = settle(score_scale * jnp.einsum('thd,shd->hts', query_h, key_h) * causal)
            grad_scores = settle(score_scale * jnp.einsum('the,she->hts', grad_h, value_h) * causal)
            query_g = jnp.einsum('hts,shd->thd', grad_scores, key_h) + jnp.einsum('the,hde->thd', grad_h, prefix_scaled)
            key_g = jnp.einsum('hts,thd->shd', grad_scores, query_h) + jnp.einsum('she,hde->shd', value_h, suffix_scaled)
            value_g = jnp.einsum('hts,the->she', scores, grad_h) + jnp.einsum('shd,hde->she', key_h, suffix_scaled)
            return (dummy, (query_g.astype(jnp.bfloat16).reshape(TOK_DEV, HD), key_g.astype(jnp.bfloat16).reshape(TOK_DEV, HD), value_g.astype(jnp.bfloat16).reshape(TOK_DEV, HD)))
        _, (query_gs, key_gs, value_gs) = lax.scan(gradients, jnp.zeros((), jnp.float32), (query_blocks, key_blocks, value_blocks, head_grads, prefixes, suffixes))
        return (query_gs.reshape(seq_length, HD), key_gs.reshape(seq_length, HD), value_gs.reshape(seq_length, HD), weight_acc)
    query_grad, key_grad, value_grad, weight_parts = lax.map(one_sequence, (queries, key_rows, value_rows, out_grad))
    return (query_grad, key_grad, value_grad, lax.optimization_barrier(jnp.sum(weight_parts, axis=0)))
```

```python
import math

import jax
import jax.numpy as jnp
from jax import lax
from jax.sharding import PartitionSpec as P

HEADS = 16
HEAD = 128
HD = 2048


def exchanged_sums(part, scale, axis, reverse):
    count = lax.axis_size(axis)
    heads, depth, width = part.shape
    rows = part.reshape(heads * depth, width).astype(jnp.bfloat16)
    mine = lax.all_to_all(rows, axis, 0, 0, tiled=True)
    mine = mine.reshape(count, -1, width).astype(jnp.float32)
    order = range(count - 1, -1, -1) if reverse else range(count)
    state = jnp.zeros_like(mine[0])
    sums = [None] * count
    for source in order:
        sums[source] = (scale * state).astype(jnp.bfloat16)
        state = state + mine[source]
    back = lax.all_to_all(jnp.concatenate(sums, axis=0), axis, 0, 0, tiled=True)
    return back.reshape(heads, depth, width)


def shards(queries, key_rows, value_rows, out_grad, out_weight):
    tokens_dev = queries.shape[1]
    seq_devices = lax.axis_size("seq")
    data_devices = lax.axis_size("dp")
    seq_length = tokens_dev * seq_devices
    seq_count = queries.shape[0] * data_devices
    score_scale = 1.0 / math.sqrt(HEAD * seq_length)
    grad_scale = 1.0 / math.sqrt(seq_count * seq_length)
    query_flat = queries[0]
    grad_flat = out_grad[0]
    query_h = query_flat.reshape(tokens_dev, HEADS, HEAD)
    key_h = key_rows[0].reshape(tokens_dev, HEADS, HEAD)
    value_h = value_rows[0].reshape(tokens_dev, HEADS, HEAD)
    row_ids = lax.broadcasted_iota(jnp.int32, (tokens_dev, tokens_dev), 0)
    col_ids = lax.broadcasted_iota(jnp.int32, (tokens_dev, tokens_dev), 1)
    causal = (row_ids >= col_ids).astype(jnp.float32)
    kv_local = jnp.einsum("shd,she->hde", key_h, value_h, preferred_element_type=jnp.float32)
    wide_weight = lax.all_gather(out_weight, "dp", axis=1, tiled=True)
    head_grad = lax.dot_general(
        grad_flat,
        lax.all_gather(wide_weight, "seq", axis=0, tiled=True),
        (((1,), (1,)), ((), ())),
        preferred_element_type=jnp.float32,
    ).astype(jnp.bfloat16)
    grad_h = head_grad.reshape(tokens_dev, HEADS, HEAD)
    query_dout = jnp.einsum("thd,the->hde", query_h, grad_h, preferred_element_type=jnp.float32)
    prefix_scaled = exchanged_sums(kv_local, score_scale, "seq", False)
    suffix_scaled = exchanged_sums(query_dout, score_scale, "seq", True)
    scores = (
        score_scale
        * jnp.einsum("thd,shd->hts", query_h, key_h, preferred_element_type=jnp.float32)
        * causal
    ).astype(jnp.bfloat16)
    attended = jnp.einsum("hts,shd->thd", scores, value_h, preferred_element_type=jnp.float32)
    attended = attended + jnp.einsum(
        "thd,hde->the", query_h, prefix_scaled, preferred_element_type=jnp.float32
    )
    attended = attended.astype(jnp.bfloat16).reshape(tokens_dev, HD)
    row_sums = lax.psum_scatter(
        (
            grad_scale
            * lax.dot_general(
                attended, grad_flat, (((0,), (0,)), ((), ())), preferred_element_type=jnp.float32
            )
        ).astype(jnp.bfloat16),
        "seq",
        scatter_dimension=0,
        tiled=True,
    )
    weight_grad = lax.psum_scatter(row_sums, "dp", scatter_dimension=1, tiled=True).astype(
        jnp.float32
    )
    grad_scores = (
        score_scale
        * jnp.einsum("the,she->hts", grad_h, value_h, preferred_element_type=jnp.float32)
        * causal
    ).astype(jnp.bfloat16)
    query_g = jnp.einsum("hts,shd->thd", grad_scores, key_h, preferred_element_type=jnp.float32)
    query_g = query_g + jnp.einsum(
        "the,hde->thd", grad_h, prefix_scaled, preferred_element_type=jnp.float32
    )
    key_g = jnp.einsum("hts,thd->shd", grad_scores, query_h, preferred_element_type=jnp.float32)
    key_g = key_g + jnp.einsum(
        "she,hde->shd", value_h, suffix_scaled, preferred_element_type=jnp.float32
    )
    value_g = jnp.einsum("hts,the->she", scores, grad_h, preferred_element_type=jnp.float32)
    value_g = value_g + jnp.einsum(
        "shd,hde->she", key_h, suffix_scaled, preferred_element_type=jnp.float32
    )
    query_grad = query_g.astype(jnp.bfloat16).reshape(1, tokens_dev, HD)
    key_grad = key_g.astype(jnp.bfloat16).reshape(1, tokens_dev, HD)
    value_grad = value_g.astype(jnp.bfloat16).reshape(1, tokens_dev, HD)
    return (query_grad, key_grad, value_grad, weight_grad)


def solution(mesh):
    return jax.shard_map(
        shards,
        mesh=mesh,
        in_specs=(
            P("dp", "seq", None),
            P("dp", "seq", None),
            P("dp", "seq", None),
            P("dp", "seq", None),
            P("seq", "dp"),
        ),
        out_specs=(
            P("dp", "seq", None),
            P("dp", "seq", None),
            P("dp", "seq", None),
            P("seq", "dp"),
        ),
        check_vma=False,
    )
```

```python
import functools
import math

import jax
import jax.numpy as jnp
from jax import lax
from jax.experimental import pallas as pl
from jax.experimental.pallas import tpu as pltpu
from jax.sharding import PartitionSpec as P

HEADS = 16
HEAD = 128
HD = 2048


def exchanged_sums(part, scale, axis, reverse):
    count = lax.axis_size(axis)
    heads, depth, width = part.shape
    rows = part.reshape(heads * depth, width).astype(jnp.bfloat16)
    mine = lax.all_to_all(rows, axis, 0, 0, tiled=True)
    mine = mine.reshape(count, -1)
    ids = jnp.arange(count)
    ahead = ids[:, None] < ids[None, :] if reverse else ids[:, None] > ids[None, :]
    sums = jnp.dot(ahead.astype(jnp.bfloat16), mine, preferred_element_type=jnp.float32)
    sums = (scale * sums).astype(jnp.bfloat16).reshape(-1, width)
    back = lax.all_to_all(sums, axis, 0, 0, tiled=True)
    return back.reshape(heads, depth, width)


STREAMS = 4
MESH = pl.DeviceIdType.MESH


def log2(count):
    return count.bit_length() - 1


def stream_bits(stream, seq_count, data_count):
    high = [("seq", bit) for bit in range(log2(seq_count) - 1, 0, -1)]
    data = [("dp", bit) for bit in range(log2(data_count))]
    return high[:-1] + data + high[-1:] if stream % 2 else high + data


def place(bits, seq, data):
    index = {"seq": seq, "dp": data}
    return sum((index[axis] // 2**bit) % 2 * 2**level for level, (axis, bit) in enumerate(bits))


def partner(axis, bit):
    index = lax.axis_index(axis)
    return {axis: index + (1 - 2 * ((index // 2**bit) % 2)) * 2**bit}


def greet(seq_count, data_count):
    barrier = pltpu.get_barrier_semaphore()
    bits = [("seq", 0)] + stream_bits(0, seq_count, data_count)
    for axis, bit in bits:
        pl.semaphore_signal(barrier, inc=1, device_id=partner(axis, bit), device_id_type=MESH)
    pl.semaphore_wait(barrier, len(bits))


def remote(src, dst, send, recv, device):
    return pltpu.make_async_remote_copy(
        src_ref=src, dst_ref=dst, send_sem=send, recv_sem=recv, device_id=device, device_id_type=MESH
    )


def head_grad_kernel(
    seq_count, data_count, weight_ref, grad_ref, out_ref,
    held, sib_grad, away, landed, send_sem, recv_sem, pair_send, pair_recv,
):
    seq, data = lax.axis_index("seq"), lax.axis_index("dp")
    core = seq % 2
    sibling = partner("seq", 0)
    rows = held.shape[2]
    orders = [stream_bits(s, seq_count, data_count) for s in range(STREAMS)]
    slots = [place(orders[s], seq, data) for s in range(STREAMS)]
    levels = len(orders[0])
    for s in range(STREAMS):
        held[s, slots[s]] = weight_ref[s * rows : (s + 1) * rows, :]
    greet(seq_count, data_count)

    def hop(s, level):
        size = 2**level
        block = held.at[s, pl.ds(slots[s] // size * size, size)]
        axis, bit = orders[s][level]
        return remote(
            block, block, send_sem.at[s, level], recv_sem.at[s, level], partner(axis, bit)
        )

    for s in range(STREAMS):
        hop(s, 0).start()
    swap = remote(grad_ref, sib_grad, pair_send.at[0], pair_recv.at[0], sibling)
    swap.start()
    for level in range(levels):
        for s in range(STREAMS):
            hop(s, level).wait()
            if level + 1 < levels:
                hop(s, level + 1).start()
    swap.wait()

    group = max(1, 256 // (rows * STREAMS))
    width = group * rows * STREAMS
    for first in range(0, seq_count // 2, group):
        panel = jnp.concatenate(
            [
                jnp.concatenate(
                    [held[s, place(orders[s], 2 * j, d)] for d in range(data_count)], axis=1
                )
                for j in range(first, first + group)
                for s in range(STREAMS)
            ],
            axis=0,
        )
        columns = slice(first // group * width, (first // group + 1) * width)
        for source, target in ((grad_ref, out_ref.at[core]), (sib_grad, away)):
            target[:, columns] = lax.dot_general(
                source[...], panel, (((1,), (1,)), ((), ())), preferred_element_type=jnp.float32
            ).astype(jnp.bfloat16)
    back = remote(away, landed, pair_send.at[1], pair_recv.at[1], sibling)
    back.start()
    back.wait()
    out_ref[1 - core] = landed[...]


def gathered_head_grad(weight, grad, seq_count, data_count):
    tokens, features = grad.shape[0], weight.shape[0] * seq_count
    levels = log2(seq_count // 2) + log2(data_count)
    half = (tokens, features // 2)
    vmem = pl.BlockSpec(memory_space=pltpu.VMEM)
    return pl.pallas_call(
        functools.partial(head_grad_kernel, seq_count, data_count),
        out_shape=jax.ShapeDtypeStruct((2,) + half, jnp.bfloat16),
        in_specs=[vmem] * 2,
        out_specs=vmem,
        scratch_shapes=[
            pltpu.VMEM(
                (STREAMS, 2**levels, weight.shape[0] // STREAMS, weight.shape[1]), jnp.bfloat16
            ),
            pltpu.VMEM(grad.shape, jnp.bfloat16),
            pltpu.VMEM(half, jnp.bfloat16),
            pltpu.VMEM(half, jnp.bfloat16),
            pltpu.SemaphoreType.DMA((STREAMS, levels)),
            pltpu.SemaphoreType.DMA((STREAMS, levels)),
            pltpu.SemaphoreType.DMA((2,)),
            pltpu.SemaphoreType.DMA((2,)),
        ],
        compiler_params=pltpu.CompilerParams(
            collective_id=0, has_side_effects=True, vmem_limit_bytes=40 << 20
        ),
        cost_estimate=pl.CostEstimate(
            flops=2 * tokens * features * grad.shape[1],
            bytes_accessed=150 << 20,
            transcendentals=0,
        ),
    )(weight, grad)


def weight_grad_kernel(
    seq_count, data_count, scale, att_ref, grad_ref, out_ref,
    sums, arrived, sib_att, sib_grad, send_sem, recv_sem, pair_send, pair_recv,
):
    seq, data = lax.axis_index("seq"), lax.axis_index("dp")
    core = seq % 2
    sibling = partner("seq", 0)
    rows, columns = sums.shape[2], sums.shape[3]
    orders = [stream_bits(s, seq_count, data_count) for s in range(STREAMS)]
    slots = [place(orders[s], seq, data) for s in range(STREAMS)]
    levels = len(orders[0])
    greet(seq_count, data_count)
    swaps = [
        remote(att_ref.at[1 - core], sib_att, pair_send.at[0], pair_recv.at[0], sibling),
        remote(grad_ref, sib_grad, pair_send.at[1], pair_recv.at[1], sibling),
    ]
    for swap in swaps:
        swap.start()
    for swap in swaps:
        swap.wait()

    group = max(1, 256 // (rows * STREAMS))
    height = group * rows * STREAMS
    for first in range(0, seq_count // 2, group):
        part = pl.ds(first * rows * STREAMS, height)
        for d in range(data_count):
            across = slice(d * columns, (d + 1) * columns)
            panel = jnp.dot(
                att_ref[core, part, :], grad_ref[:, across], preferred_element_type=jnp.float32
            )
            panel = panel + jnp.dot(
                sib_att[part, :], sib_grad[:, across], preferred_element_type=jnp.float32
            )
            panel = (scale * panel).astype(jnp.bfloat16)
            for g in range(group):
                for s in range(STREAMS):
                    top = (g * STREAMS + s) * rows
                    sums[s, place(orders[s], 2 * (first + g), d)] = panel[top : top + rows, :]

    def hop(s, level):
        size = 2**level
        mine = slots[s] // size
        theirs = mine + 1 - 2 * (mine % 2)
        axis, bit = orders[s][level]
        return remote(
            sums.at[s, pl.ds(theirs * size, size)],
            arrived.at[s, pl.ds(size, size)],
            send_sem.at[s, level],
            recv_sem.at[s, level],
            partner(axis, bit),
        )

    for s in range(STREAMS):
        hop(s, levels - 1).start()
    for level in range(levels - 1, -1, -1):
        size = 2**level
        for s in range(STREAMS):
            hop(s, level).wait()
            start = slots[s] // size * size
            if level == 0:
                out_ref[s * rows : (s + 1) * rows, :] = sums[s, slots[s]].astype(
                    jnp.float32
                ) + arrived[s, 1].astype(jnp.float32)
                continue

            @pl.loop(0, size)
            def _(step):
                total = sums[s, start + step].astype(jnp.float32) + arrived[
                    s, size + step
                ].astype(jnp.float32)
                sums[s, start + step] = total.astype(jnp.bfloat16)

            hop(s, level - 1).start()


def summed_weight_grad(att, grad, scale, seq_count, data_count):
    rows = 2 * att.shape[1] // seq_count
    columns = grad.shape[1] // data_count
    levels = log2(seq_count // 2) + log2(data_count)
    slots = (STREAMS, 2**levels, rows // STREAMS, columns)
    vmem = pl.BlockSpec(memory_space=pltpu.VMEM)
    return pl.pallas_call(
        functools.partial(weight_grad_kernel, seq_count, data_count, scale),
        out_shape=jax.ShapeDtypeStruct((rows, columns), jnp.float32),
        in_specs=[vmem] * 2,
        out_specs=vmem,
        scratch_shapes=[
            pltpu.VMEM(slots, jnp.bfloat16),
            pltpu.VMEM(slots, jnp.bfloat16),
            pltpu.VMEM(att.shape[1:], jnp.bfloat16),
            pltpu.VMEM(grad.shape, jnp.bfloat16),
            pltpu.SemaphoreType.DMA((STREAMS, levels)),
            pltpu.SemaphoreType.DMA((STREAMS, levels)),
            pltpu.SemaphoreType.DMA((2,)),
            pltpu.SemaphoreType.DMA((2,)),
        ],
        compiler_params=pltpu.CompilerParams(
            collective_id=1, has_side_effects=True, vmem_limit_bytes=40 << 20
        ),
        cost_estimate=pl.CostEstimate(
            flops=4 * att.size * grad.shape[1],
            bytes_accessed=150 << 20,
            transcendentals=0,
        ),
    )(att, grad)


def shards(queries, key_rows, value_rows, out_grad, out_weight):
    tokens_dev = queries.shape[1]
    seq_devices = lax.axis_size("seq")
    data_devices = lax.axis_size("dp")
    seq_length = tokens_dev * seq_devices
    seq_count = queries.shape[0] * data_devices
    score_scale = 1.0 / math.sqrt(HEAD * seq_length)
    grad_scale = 1.0 / math.sqrt(seq_count * seq_length)
    query_flat = queries[0]
    grad_flat = out_grad[0]
    query_h = query_flat.reshape(tokens_dev, HEADS, HEAD)
    key_h = key_rows[0].reshape(tokens_dev, HEADS, HEAD)
    value_h = value_rows[0].reshape(tokens_dev, HEADS, HEAD)
    row_ids = lax.broadcasted_iota(jnp.int32, (tokens_dev, tokens_dev), 0)
    col_ids = lax.broadcasted_iota(jnp.int32, (tokens_dev, tokens_dev), 1)
    causal = (row_ids >= col_ids).astype(jnp.float32)
    kv_local = jnp.einsum("shd,she->hde", key_h, value_h, preferred_element_type=jnp.float32)
    grad_h = gathered_head_grad(out_weight, grad_flat, seq_devices, data_devices)
    feature_rows = out_weight.shape[0]
    grad_h = grad_h.reshape(2, tokens_dev, seq_devices // 2, feature_rows)
    grad_h = grad_h.transpose(1, 2, 0, 3).reshape(tokens_dev, HEADS, HEAD)
    query_dout = jnp.einsum("thd,the->hde", query_h, grad_h, preferred_element_type=jnp.float32)
    prefix_scaled = exchanged_sums(kv_local, score_scale, "seq", False)
    suffix_scaled = exchanged_sums(query_dout, score_scale, "seq", True)
    scores = (
        score_scale
        * jnp.einsum("thd,shd->hts", query_h, key_h, preferred_element_type=jnp.float32)
        * causal
    ).astype(jnp.bfloat16)
    attended = jnp.einsum("hts,shd->thd", scores, value_h, preferred_element_type=jnp.float32)
    attended = attended + jnp.einsum(
        "thd,hde->the", query_h, prefix_scaled, preferred_element_type=jnp.float32
    )
    attended = attended.astype(jnp.bfloat16).reshape(
        tokens_dev, seq_devices // 2, 2, feature_rows
    )
    attended = attended.transpose(2, 1, 3, 0).reshape(2, HD // 2, tokens_dev)
    weight_grad = summed_weight_grad(attended, grad_flat, grad_scale, seq_devices, data_devices)
    grad_scores = (
        score_scale
        * jnp.einsum("the,she->hts", grad_h, value_h, preferred_element_type=jnp.float32)
        * causal
    ).astype(jnp.bfloat16)
    query_g = jnp.einsum("hts,shd->thd", grad_scores, key_h, preferred_element_type=jnp.float32)
    query_g = query_g + jnp.einsum(
        "the,hde->thd", grad_h, prefix_scaled, preferred_element_type=jnp.float32
    )
    key_g = jnp.einsum("hts,thd->shd", grad_scores, query_h, preferred_element_type=jnp.float32)
    key_g = key_g + jnp.einsum(
        "she,hde->shd", value_h, suffix_scaled, preferred_element_type=jnp.float32
    )
    value_g = jnp.einsum("hts,the->she", scores, grad_h, preferred_element_type=jnp.float32)
    value_g = value_g + jnp.einsum(
        "shd,hde->she", key_h, suffix_scaled, preferred_element_type=jnp.float32
    )
    query_grad = query_g.astype(jnp.bfloat16).reshape(1, tokens_dev, HD)
    key_grad = key_g.astype(jnp.bfloat16).reshape(1, tokens_dev, HD)
    value_grad = value_g.astype(jnp.bfloat16).reshape(1, tokens_dev, HD)
    return (query_grad, key_grad, value_grad, weight_grad)


def solution(mesh):
    return jax.shard_map(
        shards,
        mesh=mesh,
        in_specs=(
            P("dp", "seq", None),
            P("dp", "seq", None),
            P("dp", "seq", None),
            P("dp", "seq", None),
            P("seq", "dp"),
        ),
        out_specs=(
            P("dp", "seq", None),
            P("dp", "seq", None),
            P("dp", "seq", None),
            P("seq", "dp"),
        ),
        check_vma=False,
    )
```

```python
import functools
import math

import jax
import jax.numpy as jnp
from jax import lax
from jax.experimental import pallas as pl
from jax.experimental.pallas import tpu as pltpu
from jax.sharding import PartitionSpec as P

HEADS = 16
HEAD = 128
HD = 2048


STREAMS = 4
MESH = pl.DeviceIdType.MESH


def log2(count):
    return count.bit_length() - 1


def stream_bits(stream, seq_count, data_count):
    high = [("seq", bit) for bit in range(log2(seq_count) - 1, 0, -1)]
    data = [("dp", bit) for bit in range(log2(data_count))]
    return high[:-1] + data + high[-1:] if stream % 2 else high + data


def place(bits, seq, data):
    index = {"seq": seq, "dp": data}
    return sum((index[axis] // 2**bit) % 2 * 2**level for level, (axis, bit) in enumerate(bits))


def partner(axis, bit):
    index = lax.axis_index(axis)
    return {axis: index + (1 - 2 * ((index // 2**bit) % 2)) * 2**bit}


def greet(seq_count, data_count):
    barrier = pltpu.get_barrier_semaphore()
    bits = [("seq", 0)] + stream_bits(0, seq_count, data_count)
    for axis, bit in bits:
        pl.semaphore_signal(barrier, inc=1, device_id=partner(axis, bit), device_id_type=MESH)
    pl.semaphore_wait(barrier, len(bits))


def remote(src, dst, send, recv, device):
    return pltpu.make_async_remote_copy(
        src_ref=src, dst_ref=dst, send_sem=send, recv_sem=recv, device_id=device, device_id_type=MESH
    )


def contract(left, right, left_dim, right_dim):
    return lax.dot_general(
        left, right, (((left_dim,), (right_dim,)), ((), ())), preferred_element_type=jnp.float32
    )


def sum_steps(part, result, scale, reverse, scratch, seq_count):
    out16, in16, total, before, outs, ins, send_sem, recv_sem = scratch
    seq = lax.axis_index("seq")
    core = seq % 2
    half = before.shape[0]
    own = pl.ds(pl.multiple_of(core * half, half), half)
    other = pl.ds(pl.multiple_of((1 - core) * half, half), half)
    hops = log2(seq_count) - 1

    def flag(bit):
        set_bit = (seq // 2**bit) % 2
        return ((1 - set_bit) if reverse else set_bit).astype(jnp.float32)

    def pair_hop():
        return remote(out16, in16, send_sem.at[0], recv_sem.at[0], partner("seq", 0))

    def chip_hop(level):
        return remote(
            outs.at[level], ins.at[level], send_sem.at[level + 1], recv_sem.at[level + 1],
            partner("seq", level + 1) if level < hops else partner("seq", 0),
        )

    def first():
        out16[...] = part[...].astype(jnp.bfloat16)
        pair_hop().start()

    def second():
        pair_hop().wait()
        total[...] = part[own, :] + in16[own, :].astype(jnp.float32)
        before[...] = jnp.zeros_like(before)
        outs[0] = total[...].astype(jnp.bfloat16)
        chip_hop(0).start()

    def next_hop(level):
        chip_hop(level).wait()
        got = ins[level].astype(jnp.float32)
        before[...] += flag(level + 1) * got
        if level + 1 < hops:
            total[...] += got
            outs[level + 1] = total[...].astype(jnp.bfloat16)
        else:
            outs[level + 1] = before[...].astype(jnp.bfloat16)
        chip_hop(level + 1).start()

    def last():
        chip_hop(hops).wait()
        result[own, :] = (
            scale * (before[...] + flag(0) * in16[own, :].astype(jnp.float32))
        ).astype(jnp.bfloat16)
        result[other, :] = (
            scale
            * (ins[hops].astype(jnp.float32) + flag(0) * in16[other, :].astype(jnp.float32))
        ).astype(jnp.bfloat16)

    return [first, second] + [functools.partial(next_hop, level) for level in range(hops)] + [last]


def kernel(
    seq_count, data_count, score_scale, grad_scale,
    query_ref, key_ref, value_ref, grad_ref, weight_ref,
    query_out, key_out, value_out, weight_out,
    held, sums, arrived, sib_grad, head_grad, away, landed, att, sib_att,
    scores, key_sum, value_sum, part, prefix, suffix,
    out16, in16, total, before, outs, ins,
    gather_send, gather_recv, reduce_send, reduce_recv, pair_send, pair_recv,
    scan_send, scan_recv,
):
    seq, data = lax.axis_index("seq"), lax.axis_index("dp")
    core = seq % 2
    sibling = partner("seq", 0)
    rows, columns = held.shape[2], held.shape[3]
    tokens = grad_ref.shape[0]
    shard_rows = rows * STREAMS
    orders = [stream_bits(s, seq_count, data_count) for s in range(STREAMS)]
    slots = [place(orders[s], seq, data) for s in range(STREAMS)]
    levels = len(orders[0])
    group = max(1, 256 // shard_rows)
    causal = (
        lax.broadcasted_iota(jnp.int32, (tokens, tokens), 0)
        >= lax.broadcasted_iota(jnp.int32, (tokens, tokens), 1)
    ).astype(jnp.float32)

    def head_columns(h):
        return pl.ds(pl.multiple_of(h * HEAD, HEAD), HEAD)

    for s in range(STREAMS):
        held[s, slots[s]] = weight_ref[s * rows : (s + 1) * rows, :]
    greet(seq_count, data_count)

    def gather_hop(s, level):
        size = 2**level
        block = held.at[s, pl.ds(slots[s] // size * size, size)]
        axis, bit = orders[s][level]
        return remote(
            block, block, gather_send.at[s, level], gather_recv.at[s, level], partner(axis, bit)
        )

    def gather_level(level):
        for s in range(STREAMS):
            gather_hop(s, level).wait()
            if level + 1 < levels:
                gather_hop(s, level + 1).start()

    def reduce_hop(s, level):
        size = 2**level
        mine = slots[s] // size
        theirs = mine + 1 - 2 * (mine % 2)
        axis, bit = orders[s][level]
        return remote(
            sums.at[s, pl.ds(theirs * size, size)],
            arrived.at[s, pl.ds(size, size)],
            reduce_send.at[s, level],
            reduce_recv.at[s, level],
            partner(axis, bit),
        )

    def reduce_level(level):
        size = 2**level
        for s in range(STREAMS):
            reduce_hop(s, level).wait()
            start = slots[s] // size * size
            if level == 0:
                weight_out[s * rows : (s + 1) * rows, :] = sums[s, slots[s]].astype(
                    jnp.float32
                ) + arrived[s, 1].astype(jnp.float32)
                continue

            @pl.loop(0, size)
            def _(step):
                added = sums[s, start + step].astype(jnp.float32) + arrived[
                    s, size + step
                ].astype(jnp.float32)
                sums[s, start + step] = added.astype(jnp.bfloat16)

            reduce_hop(s, level - 1).start()

    def swap(src, dst, index):
        return remote(src, dst, pair_send.at[index], pair_recv.at[index], sibling)

    for s in range(STREAMS):
        gather_hop(s, 0).start()
    grad_swap = swap(grad_ref, sib_grad, 0)
    grad_swap.start()

    @pl.loop(0, HEADS)
    def _(h):
        at = head_columns(h)
        part[at, :] = contract(key_ref[:, at], value_ref[:, at], 0, 0)

    scan = (out16, in16, total, before, outs, ins)
    steps = sum_steps(
        part, prefix, score_scale, False,
        tuple(ref.at[0] for ref in scan + (scan_send, scan_recv)), seq_count,
    )
    steps[0]()

    @pl.loop(0, HEADS)
    def _(h):
        at = head_columns(h)
        scores[h] = (
            score_scale * contract(query_ref[:, at], key_ref[:, at], 1, 1) * causal
        ).astype(jnp.bfloat16)

    for index in range(max(len(steps) - 1, levels - 1)):
        if index + 1 < len(steps):
            steps[index + 1]()
        if index < levels - 1:
            gather_level(index)

    @pl.loop(0, HEADS)
    def _(h):
        at = head_columns(h)
        attended = contract(scores[h], value_ref[:, at], 1, 0)
        attended = attended + contract(query_ref[:, at], prefix[at, :], 1, 0)
        turned = attended.T.astype(jnp.bfloat16)
        pieces = HEAD // shard_rows
        for piece in range(pieces):
            shard = h * pieces + piece
            att[shard % 2, pl.ds(pl.multiple_of(shard // 2 * shard_rows, shard_rows), shard_rows), :] = (
                turned[piece * shard_rows : (piece + 1) * shard_rows, :]
            )

    att_swap = swap(att.at[1 - core], sib_att, 1)
    att_swap.start()
    grad_swap.wait()
    att_swap.wait()
    height = group * shard_rows
    for first in range(0, seq_count // 2, group):
        strip = pl.ds(first * shard_rows, height)
        for d in range(data_count):
            across = slice(d * columns, (d + 1) * columns)
            panel = contract(att[core, strip, :], grad_ref[:, across], 1, 0)
            panel = panel + contract(sib_att[strip, :], sib_grad[:, across], 1, 0)
            panel = (grad_scale * panel).astype(jnp.bfloat16)
            for g in range(group):
                for s in range(STREAMS):
                    top = (g * STREAMS + s) * rows
                    sums[s, place(orders[s], 2 * (first + g), d)] = panel[top : top + rows, :]
    for s in range(STREAMS):
        reduce_hop(s, levels - 1).start()

    gather_level(levels - 1)
    half = away.shape[1]
    for first in range(0, seq_count // 2, group):
        panel = jnp.concatenate(
            [
                jnp.concatenate(
                    [held[s, place(orders[s], 2 * j, d)] for d in range(data_count)], axis=1
                )
                for j in range(first, first + group)
                for s in range(STREAMS)
            ],
            axis=0,
        )
        strip = slice(first * shard_rows, first * shard_rows + height)
        away[:, strip] = contract(sib_grad[...], panel, 1, 1).astype(jnp.bfloat16)
        mine = contract(grad_ref[...], panel, 1, 1).astype(jnp.bfloat16)
        for side in range(2):

            @pl.when(core == side)
            def _():
                for g in range(group):
                    left = (2 * (first + g) + side) * shard_rows
                    head_grad[:, left : left + shard_rows] = mine[
                        :, g * shard_rows : (g + 1) * shard_rows
                    ]

    back = swap(away, landed, 2)
    back.start()
    back.wait()
    for side in range(2):

        @pl.when(core != side)
        def _():
            for j in range(seq_count // 2):
                left = (2 * j + side) * shard_rows
                head_grad[:, left : left + shard_rows] = landed[
                    :, j * shard_rows : (j + 1) * shard_rows
                ]

    @pl.loop(0, HEADS)
    def _(h):
        at = head_columns(h)
        part[at, :] = contract(query_ref[:, at], head_grad[:, at], 0, 0)

    steps = sum_steps(
        part, suffix, score_scale, True,
        tuple(ref.at[1] for ref in scan + (scan_send, scan_recv)), seq_count,
    )
    steps[0]()

    def local_heads(begin, end):
        @pl.loop(begin, end)
        def _(h):
            at = head_columns(h)
            rows_g, rows_q, rows_k = head_grad[:, at], query_ref[:, at], key_ref[:, at]
            grad_scores = (
                score_scale * contract(rows_g, value_ref[:, at], 1, 1) * causal
            ).astype(jnp.bfloat16)
            query_out[:, at] = (
                contract(grad_scores, rows_k, 1, 0) + contract(rows_g, prefix[at, :], 1, 1)
            ).astype(jnp.bfloat16)
            key_sum[:, at] = contract(grad_scores, rows_q, 0, 0)
            value_sum[:, at] = contract(scores[h], rows_g, 0, 0)

    chunks = len(steps) - 1
    for index in range(max(chunks, levels - 1)):
        if index < chunks:
            local_heads(HEADS * index // chunks, HEADS * (index + 1) // chunks)
            steps[index + 1]()
        if index < levels - 1:
            reduce_level(levels - 1 - index)

    @pl.loop(0, HEADS)
    def _(h):
        at = head_columns(h)
        key_out[:, at] = (
            key_sum[:, at] + contract(value_ref[:, at], suffix[at, :], 1, 1)
        ).astype(jnp.bfloat16)
        value_out[:, at] = (
            value_sum[:, at] + contract(key_ref[:, at], suffix[at, :], 1, 0)
        ).astype(jnp.bfloat16)

    reduce_level(0)


def shards(queries, key_rows, value_rows, out_grad, out_weight):
    tokens = queries.shape[1]
    seq_count = lax.axis_size("seq")
    data_count = lax.axis_size("dp")
    seq_length = tokens * seq_count
    score_scale = 1.0 / math.sqrt(HEAD * seq_length)
    grad_scale = 1.0 / math.sqrt(queries.shape[0] * data_count * seq_length)
    features = queries.shape[2]
    shard_rows, columns = out_weight.shape
    width = out_grad.shape[2]
    hops = log2(seq_count // 2)
    levels = hops + log2(data_count)
    bf16, f32 = jnp.bfloat16, jnp.float32
    blocks = (STREAMS, 2**levels, shard_rows // STREAMS, columns)
    half = features // 2
    vmem = pl.BlockSpec(memory_space=pltpu.VMEM)
    dma = pltpu.SemaphoreType.DMA
    flat = jax.ShapeDtypeStruct((tokens, features), bf16)
    query_grad, key_grad, value_grad, weight_grad = pl.pallas_call(
        functools.partial(kernel, seq_count, data_count, score_scale, grad_scale),
        out_shape=(flat, flat, flat, jax.ShapeDtypeStruct((shard_rows, columns), f32)),
        in_specs=[vmem] * 5,
        out_specs=(vmem,) * 4,
        scratch_shapes=[
            pltpu.VMEM(blocks, bf16),
            pltpu.VMEM(blocks, bf16),
            pltpu.VMEM(blocks, bf16),
            pltpu.VMEM((tokens, width), bf16),
            pltpu.VMEM((tokens, features), bf16),
            pltpu.VMEM((tokens, half), bf16),
            pltpu.VMEM((tokens, half), bf16),
            pltpu.VMEM((2, half, tokens), bf16),
            pltpu.VMEM((half, tokens), bf16),
            pltpu.VMEM((HEADS, tokens, tokens), bf16),
            pltpu.VMEM((tokens, features), f32),
            pltpu.VMEM((tokens, features), f32),
            pltpu.VMEM((features, HEAD), f32),
            pltpu.VMEM((features, HEAD), bf16),
            pltpu.VMEM((features, HEAD), bf16),
            pltpu.VMEM((2, features, HEAD), bf16),
            pltpu.VMEM((2, features, HEAD), bf16),
            pltpu.VMEM((2, half, HEAD), f32),
            pltpu.VMEM((2, half, HEAD), f32),
            pltpu.VMEM((2, hops + 1, half, HEAD), bf16),
            pltpu.VMEM((2, hops + 1, half, HEAD), bf16),
            dma((STREAMS, levels)),
            dma((STREAMS, levels)),
            dma((STREAMS, levels)),
            dma((STREAMS, levels)),
            dma((3,)),
            dma((3,)),
            dma((2, hops + 2)),
            dma((2, hops + 2)),
        ],
        compiler_params=pltpu.CompilerParams(
            collective_id=0, has_side_effects=True, vmem_limit_bytes=56 << 20
        ),
    )(queries[0], key_rows[0], value_rows[0], out_grad[0], out_weight)
    return query_grad[None], key_grad[None], value_grad[None], weight_grad


def solution(mesh):
    return jax.shard_map(
        shards,
        mesh=mesh,
        in_specs=(
            P("dp", "seq", None),
            P("dp", "seq", None),
            P("dp", "seq", None),
            P("dp", "seq", None),
            P("seq", "dp"),
        ),
        out_specs=(
            P("dp", "seq", None),
            P("dp", "seq", None),
            P("dp", "seq", None),
            P("seq", "dp"),
        ),
        check_vma=False,
    )
```

```python
import functools
import math

import jax
import jax.numpy as jnp
from jax import lax
from jax.experimental import pallas as pl
from jax.experimental.pallas import tpu as pltpu
from jax.sharding import PartitionSpec as P

HEADS = 16
HEAD = 128
HD = 2048


STREAMS = 4
MESH = pl.DeviceIdType.MESH


def log2(count):
    return count.bit_length() - 1


def stream_bits(stream, seq_count, data_count):
    high = [("seq", bit) for bit in range(log2(seq_count) - 1, 0, -1)]
    data = [("dp", bit) for bit in range(log2(data_count))]
    far, near = high[:-1], high[-1:]
    return [high + data, far + data + near, near + data + far, data + high][stream % 4]


def place(bits, seq, data):
    index = {"seq": seq, "dp": data}
    return sum((index[axis] // 2**bit) % 2 * 2**level for level, (axis, bit) in enumerate(bits))


def partner(axis, bit):
    index = lax.axis_index(axis)
    return {axis: index + (1 - 2 * ((index // 2**bit) % 2)) * 2**bit}


def greet(seq_count, data_count):
    barrier = pltpu.get_barrier_semaphore()
    bits = [("seq", 0)] + stream_bits(0, seq_count, data_count)
    for axis, bit in bits:
        pl.semaphore_signal(barrier, inc=1, device_id=partner(axis, bit), device_id_type=MESH)
    pl.semaphore_wait(barrier, len(bits))


def remote(src, dst, send, recv, device):
    return pltpu.make_async_remote_copy(
        src_ref=src, dst_ref=dst, send_sem=send, recv_sem=recv, device_id=device, device_id_type=MESH
    )


def contract(left, right, left_dim, right_dim):
    return lax.dot_general(
        left, right, (((left_dim,), (right_dim,)), ((), ())), preferred_element_type=jnp.float32
    )


def sum_steps(part, result, scale, reverse, scratch, seq_count):
    out16, in16, total, before, outs, ins, send_sem, recv_sem = scratch
    seq = lax.axis_index("seq")
    core = seq % 2
    half = before.shape[0]
    own = pl.ds(pl.multiple_of(core * half, half), half)
    other = pl.ds(pl.multiple_of((1 - core) * half, half), half)
    hops = log2(seq_count) - 1

    def flag(bit):
        set_bit = (seq // 2**bit) % 2
        return ((1 - set_bit) if reverse else set_bit).astype(jnp.float32)

    def pair_hop():
        return remote(out16, in16, send_sem.at[0], recv_sem.at[0], partner("seq", 0))

    def chip_hop(level):
        return remote(
            outs.at[level], ins.at[level], send_sem.at[level + 1], recv_sem.at[level + 1],
            partner("seq", level + 1) if level < hops else partner("seq", 0),
        )

    def first():
        out16[...] = part[...].astype(jnp.bfloat16)
        pair_hop().start()

    def second():
        pair_hop().wait()
        total[...] = part[own, :] + in16[own, :].astype(jnp.float32)
        before[...] = jnp.zeros_like(before)
        outs[0] = total[...].astype(jnp.bfloat16)
        chip_hop(0).start()

    def next_hop(level):
        chip_hop(level).wait()
        got = ins[level].astype(jnp.float32)
        before[...] += flag(level + 1) * got
        if level + 1 < hops:
            total[...] += got
            outs[level + 1] = total[...].astype(jnp.bfloat16)
        else:
            outs[level + 1] = before[...].astype(jnp.bfloat16)
        chip_hop(level + 1).start()

    def last():
        chip_hop(hops).wait()
        result[own, :] = (
            scale * (before[...] + flag(0) * in16[own, :].astype(jnp.float32))
        ).astype(jnp.bfloat16)
        result[other, :] = (
            scale
            * (ins[hops].astype(jnp.float32) + flag(0) * in16[other, :].astype(jnp.float32))
        ).astype(jnp.bfloat16)

    return [first, second] + [functools.partial(next_hop, level) for level in range(hops)] + [last]


def kernel(
    seq_count, data_count, score_scale, grad_scale,
    query_ref, key_ref, value_ref, grad_ref, weight_ref,
    query_out, key_out, value_out, weight_out,
    held, sums, arrived, sib_grad, head_grad, away, landed, att, sib_att,
    scores, key_sum, value_sum, part, prefix, suffix,
    out16, in16, total, before, outs, ins,
    gather_send, gather_recv, reduce_send, reduce_recv, pair_send, pair_recv,
    scan_send, scan_recv,
):
    seq, data = lax.axis_index("seq"), lax.axis_index("dp")
    core = seq % 2
    sibling = partner("seq", 0)
    rows, columns = held.shape[2], held.shape[3]
    tokens = grad_ref.shape[0]
    shard_rows = rows * STREAMS
    orders = [stream_bits(s, seq_count, data_count) for s in range(STREAMS)]
    slots = [place(orders[s], seq, data) for s in range(STREAMS)]
    levels = len(orders[0])
    group = max(1, 256 // shard_rows)
    causal = (
        lax.broadcasted_iota(jnp.int32, (tokens, tokens), 0)
        >= lax.broadcasted_iota(jnp.int32, (tokens, tokens), 1)
    ).astype(jnp.float32)

    def head_columns(h):
        return pl.ds(pl.multiple_of(h * HEAD, HEAD), HEAD)

    for s in range(STREAMS):
        held[s, slots[s]] = weight_ref[s * rows : (s + 1) * rows, :]
    greet(seq_count, data_count)

    def gather_hop(s, level):
        size = 2**level
        block = held.at[s, pl.ds(slots[s] // size * size, size)]
        axis, bit = orders[s][level]
        return remote(
            block, block, gather_send.at[s, level], gather_recv.at[s, level], partner(axis, bit)
        )

    def gather_level(level):
        for s in range(STREAMS):
            gather_hop(s, level).wait()
            if level + 1 < levels:
                gather_hop(s, level + 1).start()

    def reduce_hop(s, level):
        size = 2**level
        mine = slots[s] // size
        theirs = mine + 1 - 2 * (mine % 2)
        axis, bit = orders[s][level]
        return remote(
            sums.at[s, pl.ds(theirs * size, size)],
            arrived.at[s, pl.ds(size, size)],
            reduce_send.at[s, level],
            reduce_recv.at[s, level],
            partner(axis, bit),
        )

    def reduce_level(level):
        size = 2**level
        for s in range(STREAMS):
            reduce_hop(s, level).wait()
            start = slots[s] // size * size
            if level == 0:
                weight_out[s * rows : (s + 1) * rows, :] = sums[s, slots[s]].astype(
                    jnp.float32
                ) + arrived[s, 1].astype(jnp.float32)
                continue

            @pl.loop(0, size)
            def _(step):
                added = sums[s, start + step].astype(jnp.float32) + arrived[
                    s, size + step
                ].astype(jnp.float32)
                sums[s, start + step] = added.astype(jnp.bfloat16)

            reduce_hop(s, level - 1).start()

    def swap(src, dst, index):
        return remote(src, dst, pair_send.at[index], pair_recv.at[index], sibling)

    for s in range(STREAMS):
        gather_hop(s, 0).start()
    grad_swap = swap(grad_ref, sib_grad, 0)
    grad_swap.start()

    @pl.loop(0, HEADS)
    def _(h):
        at = head_columns(h)
        part[at, :] = contract(key_ref[:, at], value_ref[:, at], 0, 0)

    scan = (out16, in16, total, before, outs, ins)
    steps = sum_steps(
        part, prefix, score_scale, False,
        tuple(ref.at[0] for ref in scan + (scan_send, scan_recv)), seq_count,
    )
    steps[0]()

    @pl.loop(0, HEADS)
    def _(h):
        at = head_columns(h)
        scores[h] = (
            score_scale * contract(query_ref[:, at], key_ref[:, at], 1, 1) * causal
        ).astype(jnp.bfloat16)

    for index in range(max(len(steps) - 1, levels - 1)):
        if index + 1 < len(steps):
            steps[index + 1]()
        if index < levels - 1:
            gather_level(index)

    @pl.loop(0, HEADS)
    def _(h):
        at = head_columns(h)
        attended = contract(scores[h], value_ref[:, at], 1, 0)
        attended = attended + contract(query_ref[:, at], prefix[at, :], 1, 0)
        turned = attended.T.astype(jnp.bfloat16)
        pieces = HEAD // shard_rows
        for piece in range(pieces):
            shard = h * pieces + piece
            att[shard % 2, pl.ds(pl.multiple_of(shard // 2 * shard_rows, shard_rows), shard_rows), :] = (
                turned[piece * shard_rows : (piece + 1) * shard_rows, :]
            )

    att_swap = swap(att.at[1 - core], sib_att, 1)
    att_swap.start()
    grad_swap.wait()
    att_swap.wait()
    height = group * shard_rows
    for first in range(0, seq_count // 2, group):
        strip = pl.ds(first * shard_rows, height)
        for d in range(data_count):
            across = slice(d * columns, (d + 1) * columns)
            panel = contract(att[core, strip, :], grad_ref[:, across], 1, 0)
            panel = panel + contract(sib_att[strip, :], sib_grad[:, across], 1, 0)
            panel = (grad_scale * panel).astype(jnp.bfloat16)
            for g in range(group):
                for s in range(STREAMS):
                    top = (g * STREAMS + s) * rows
                    sums[s, place(orders[s], 2 * (first + g), d)] = panel[top : top + rows, :]
    for s in range(STREAMS):
        reduce_hop(s, levels - 1).start()

    gather_level(levels - 1)
    half = away.shape[1]
    for first in range(0, seq_count // 2, group):
        panel = jnp.concatenate(
            [
                jnp.concatenate(
                    [held[s, place(orders[s], 2 * j, d)] for d in range(data_count)], axis=1
                )
                for j in range(first, first + group)
                for s in range(STREAMS)
            ],
            axis=0,
        )
        strip = slice(first * shard_rows, first * shard_rows + height)
        away[:, strip] = contract(sib_grad[...], panel, 1, 1).astype(jnp.bfloat16)
        mine = contract(grad_ref[...], panel, 1, 1).astype(jnp.bfloat16)
        for side in range(2):

            @pl.when(core == side)
            def _():
                for g in range(group):
                    left = (2 * (first + g) + side) * shard_rows
                    head_grad[:, left : left + shard_rows] = mine[
                        :, g * shard_rows : (g + 1) * shard_rows
                    ]

    back = swap(away, landed, 2)
    back.start()
    back.wait()
    for side in range(2):

        @pl.when(core != side)
        def _():
            for j in range(seq_count // 2):
                left = (2 * j + side) * shard_rows
                head_grad[:, left : left + shard_rows] = landed[
                    :, j * shard_rows : (j + 1) * shard_rows
                ]

    @pl.loop(0, HEADS)
    def _(h):
        at = head_columns(h)
        part[at, :] = contract(query_ref[:, at], head_grad[:, at], 0, 0)

    steps = sum_steps(
        part, suffix, score_scale, True,
        tuple(ref.at[1] for ref in scan + (scan_send, scan_recv)), seq_count,
    )
    steps[0]()

    def local_heads(begin, end):
        @pl.loop(begin, end)
        def _(h):
            at = head_columns(h)
            rows_g, rows_q, rows_k = head_grad[:, at], query_ref[:, at], key_ref[:, at]
            grad_scores = (
                score_scale * contract(rows_g, value_ref[:, at], 1, 1) * causal
            ).astype(jnp.bfloat16)
            query_out[:, at] = (
                contract(grad_scores, rows_k, 1, 0) + contract(rows_g, prefix[at, :], 1, 1)
            ).astype(jnp.bfloat16)
            key_sum[:, at] = contract(grad_scores, rows_q, 0, 0)
            value_sum[:, at] = contract(scores[h], rows_g, 0, 0)

    chunks = len(steps) - 1
    for index in range(max(chunks, levels - 1)):
        if index < chunks:
            local_heads(HEADS * index // chunks, HEADS * (index + 1) // chunks)
            steps[index + 1]()
        if index < levels - 1:
            reduce_level(levels - 1 - index)

    @pl.loop(0, HEADS)
    def _(h):
        at = head_columns(h)
        key_out[:, at] = (
            key_sum[:, at] + contract(value_ref[:, at], suffix[at, :], 1, 1)
        ).astype(jnp.bfloat16)
        value_out[:, at] = (
            value_sum[:, at] + contract(key_ref[:, at], suffix[at, :], 1, 0)
        ).astype(jnp.bfloat16)

    reduce_level(0)


def shards(queries, key_rows, value_rows, out_grad, out_weight):
    tokens = queries.shape[1]
    seq_count = lax.axis_size("seq")
    data_count = lax.axis_size("dp")
    seq_length = tokens * seq_count
    score_scale = 1.0 / math.sqrt(HEAD * seq_length)
    grad_scale = 1.0 / math.sqrt(queries.shape[0] * data_count * seq_length)
    features = queries.shape[2]
    shard_rows, columns = out_weight.shape
    width = out_grad.shape[2]
    hops = log2(seq_count // 2)
    levels = hops + log2(data_count)
    bf16, f32 = jnp.bfloat16, jnp.float32
    blocks = (STREAMS, 2**levels, shard_rows // STREAMS, columns)
    half = features // 2
    vmem = pl.BlockSpec(memory_space=pltpu.VMEM)
    dma = pltpu.SemaphoreType.DMA
    flat = jax.ShapeDtypeStruct((tokens, features), bf16)
    query_grad, key_grad, value_grad, weight_grad = pl.pallas_call(
        functools.partial(kernel, seq_count, data_count, score_scale, grad_scale),
        out_shape=(flat, flat, flat, jax.ShapeDtypeStruct((shard_rows, columns), f32)),
        in_specs=[vmem] * 5,
        out_specs=(vmem,) * 4,
        scratch_shapes=[
            pltpu.VMEM(blocks, bf16),
            pltpu.VMEM(blocks, bf16),
            pltpu.VMEM(blocks, bf16),
            pltpu.VMEM((tokens, width), bf16),
            pltpu.VMEM((tokens, features), bf16),
            pltpu.VMEM((tokens, half), bf16),
            pltpu.VMEM((tokens, half), bf16),
            pltpu.VMEM((2, half, tokens), bf16),
            pltpu.VMEM((half, tokens), bf16),
            pltpu.VMEM((HEADS, tokens, tokens), bf16),
            pltpu.VMEM((tokens, features), f32),
            pltpu.VMEM((tokens, features), f32),
            pltpu.VMEM((features, HEAD), f32),
            pltpu.VMEM((features, HEAD), bf16),
            pltpu.VMEM((features, HEAD), bf16),
            pltpu.VMEM((2, features, HEAD), bf16),
            pltpu.VMEM((2, features, HEAD), bf16),
            pltpu.VMEM((2, half, HEAD), f32),
            pltpu.VMEM((2, half, HEAD), f32),
            pltpu.VMEM((2, hops + 1, half, HEAD), bf16),
            pltpu.VMEM((2, hops + 1, half, HEAD), bf16),
            dma((STREAMS, levels)),
            dma((STREAMS, levels)),
            dma((STREAMS, levels)),
            dma((STREAMS, levels)),
            dma((3,)),
            dma((3,)),
            dma((2, hops + 2)),
            dma((2, hops + 2)),
        ],
        compiler_params=pltpu.CompilerParams(
            collective_id=0, has_side_effects=True, vmem_limit_bytes=56 << 20
        ),
    )(queries[0], key_rows[0], value_rows[0], out_grad[0], out_weight)
    return query_grad[None], key_grad[None], value_grad[None], weight_grad


def solution(mesh):
    return jax.shard_map(
        shards,
        mesh=mesh,
        in_specs=(
            P("dp", "seq", None),
            P("dp", "seq", None),
            P("dp", "seq", None),
            P("dp", "seq", None),
            P("seq", "dp"),
        ),
        out_specs=(
            P("dp", "seq", None),
            P("dp", "seq", None),
            P("dp", "seq", None),
            P("seq", "dp"),
        ),
        check_vma=False,
    )
```

```python
import functools
import math

import jax
import jax.numpy as jnp
from jax import lax
from jax.experimental import pallas as pl
from jax.experimental.pallas import tpu as pltpu
from jax.sharding import PartitionSpec as P

HEADS = 16
HEAD = 128
HD = 2048


STREAMS = 4
MESH = pl.DeviceIdType.MESH


def log2(count):
    return count.bit_length() - 1


def stream_bits(stream, seq_count, data_count):
    high = [("seq", bit) for bit in range(log2(seq_count) - 1, 0, -1)]
    data = [("dp", bit) for bit in range(log2(data_count))]
    far, near = high[:-1], high[-1:]
    return [high + data, far + data + near, near + data + far, data + high][stream % 4]


def place(bits, seq, data):
    index = {"seq": seq, "dp": data}
    return sum((index[axis] // 2**bit) % 2 * 2**level for level, (axis, bit) in enumerate(bits))


def partner(axis, bit):
    index = lax.axis_index(axis)
    return {axis: index + (1 - 2 * ((index // 2**bit) % 2)) * 2**bit}


def greet(seq_count, data_count):
    barrier = pltpu.get_barrier_semaphore()
    bits = [("seq", 0)] + stream_bits(0, seq_count, data_count)
    for axis, bit in bits:
        pl.semaphore_signal(barrier, inc=1, device_id=partner(axis, bit), device_id_type=MESH)
    pl.semaphore_wait(barrier, len(bits))


def remote(src, dst, send, recv, device):
    return pltpu.make_async_remote_copy(
        src_ref=src, dst_ref=dst, send_sem=send, recv_sem=recv, device_id=device, device_id_type=MESH
    )


def contract(left, right, left_dim, right_dim):
    return lax.dot_general(
        left, right, (((left_dim,), (right_dim,)), ((), ())), preferred_element_type=jnp.float32
    )


def each_head(begin, end, together, body):
    whole = begin + (end - begin) // together * together

    @pl.loop(begin, whole, step=together)
    def _(h):
        for store in [body(h + i) for i in range(together)]:
            store()

    for store in [body(h) for h in range(whole, end)]:
        store()


def sum_steps(part, result, scale, reverse, scratch, seq_count):
    out16, in16, total, before, outs, ins, send_sem, recv_sem = scratch
    seq = lax.axis_index("seq")
    core = seq % 2
    half = before.shape[0]
    own = pl.ds(pl.multiple_of(core * half, half), half)
    other = pl.ds(pl.multiple_of((1 - core) * half, half), half)
    hops = log2(seq_count) - 1

    def flag(bit):
        set_bit = (seq // 2**bit) % 2
        return ((1 - set_bit) if reverse else set_bit).astype(jnp.float32)

    def pair_hop():
        return remote(out16, in16, send_sem.at[0], recv_sem.at[0], partner("seq", 0))

    def chip_hop(level):
        return remote(
            outs.at[level], ins.at[level], send_sem.at[level + 1], recv_sem.at[level + 1],
            partner("seq", level + 1) if level < hops else partner("seq", 0),
        )

    def first():
        out16[...] = part[...].astype(jnp.bfloat16)
        pair_hop().start()

    def second():
        pair_hop().wait()
        total[...] = part[own, :] + in16[own, :].astype(jnp.float32)
        before[...] = jnp.zeros_like(before)
        outs[0] = total[...].astype(jnp.bfloat16)
        chip_hop(0).start()

    def next_hop(level):
        chip_hop(level).wait()
        got = ins[level].astype(jnp.float32)
        before[...] += flag(level + 1) * got
        if level + 1 < hops:
            total[...] += got
            outs[level + 1] = total[...].astype(jnp.bfloat16)
        else:
            outs[level + 1] = before[...].astype(jnp.bfloat16)
        chip_hop(level + 1).start()

    def last():
        chip_hop(hops).wait()
        result[own, :] = (
            scale * (before[...] + flag(0) * in16[own, :].astype(jnp.float32))
        ).astype(jnp.bfloat16)
        result[other, :] = (
            scale
            * (ins[hops].astype(jnp.float32) + flag(0) * in16[other, :].astype(jnp.float32))
        ).astype(jnp.bfloat16)

    return [first, second] + [functools.partial(next_hop, level) for level in range(hops)] + [last]


def kernel(
    seq_count, data_count, score_scale, grad_scale,
    query_ref, key_ref, value_ref, grad_ref, weight_ref,
    query_out, key_out, value_out, weight_out,
    held, sums, arrived, sib_grad, head_grad, away, landed, att, sib_att,
    scores, key_sum, value_sum, part, prefix, suffix,
    out16, in16, total, before, outs, ins,
    gather_send, gather_recv, reduce_send, reduce_recv, pair_send, pair_recv,
    scan_send, scan_recv,
):
    seq, data = lax.axis_index("seq"), lax.axis_index("dp")
    core = seq % 2
    sibling = partner("seq", 0)
    rows, columns = held.shape[2], held.shape[3]
    tokens = grad_ref.shape[0]
    shard_rows = rows * STREAMS
    orders = [stream_bits(s, seq_count, data_count) for s in range(STREAMS)]
    slots = [place(orders[s], seq, data) for s in range(STREAMS)]
    levels = len(orders[0])
    group = max(1, 256 // shard_rows)
    causal = (
        lax.broadcasted_iota(jnp.int32, (tokens, tokens), 0)
        >= lax.broadcasted_iota(jnp.int32, (tokens, tokens), 1)
    ).astype(jnp.float32)

    def head_columns(h):
        return pl.ds(h * HEAD if isinstance(h, int) else pl.multiple_of(h * HEAD, HEAD), HEAD)

    for s in range(STREAMS):
        held[s, slots[s]] = weight_ref[s * rows : (s + 1) * rows, :]
    greet(seq_count, data_count)

    def gather_hop(s, level):
        size = 2**level
        block = held.at[s, pl.ds(slots[s] // size * size, size)]
        axis, bit = orders[s][level]
        return remote(
            block, block, gather_send.at[s, level], gather_recv.at[s, level], partner(axis, bit)
        )

    def gather_level(level):
        for s in range(STREAMS):
            gather_hop(s, level).wait()
            if level + 1 < levels:
                gather_hop(s, level + 1).start()

    def reduce_hop(s, level):
        size = 2**level
        mine = slots[s] // size
        theirs = mine + 1 - 2 * (mine % 2)
        axis, bit = orders[s][level]
        return remote(
            sums.at[s, pl.ds(theirs * size, size)],
            arrived.at[s, pl.ds(size, size)],
            reduce_send.at[s, level],
            reduce_recv.at[s, level],
            partner(axis, bit),
        )

    def reduce_level(level):
        size = 2**level
        for s in range(STREAMS):
            reduce_hop(s, level).wait()
            start = slots[s] // size * size
            if level == 0:
                weight_out[s * rows : (s + 1) * rows, :] = sums[s, slots[s]].astype(
                    jnp.float32
                ) + arrived[s, 1].astype(jnp.float32)
                continue

            @pl.loop(0, size)
            def _(step):
                added = sums[s, start + step].astype(jnp.float32) + arrived[
                    s, size + step
                ].astype(jnp.float32)
                sums[s, start + step] = added.astype(jnp.bfloat16)

            reduce_hop(s, level - 1).start()

    def swap(src, dst, index):
        return remote(src, dst, pair_send.at[index], pair_recv.at[index], sibling)

    for s in range(STREAMS):
        gather_hop(s, 0).start()
    grad_swap = swap(grad_ref, sib_grad, 0)
    grad_swap.start()

    def store(ref, index, value):
        ref[index] = value

    def key_value(h):
        at = head_columns(h)
        product = contract(key_ref[:, at], value_ref[:, at], 0, 0)
        return functools.partial(store, part, (at, slice(None)), product)

    each_head(0, HEADS, 4, key_value)

    scan = (out16, in16, total, before, outs, ins)
    steps = sum_steps(
        part, prefix, score_scale, False,
        tuple(ref.at[0] for ref in scan + (scan_send, scan_recv)), seq_count,
    )
    steps[0]()

    def head_scores(h):
        at = head_columns(h)
        product = score_scale * contract(query_ref[:, at], key_ref[:, at], 1, 1) * causal
        return functools.partial(store, scores, h, product.astype(jnp.bfloat16))

    each_head(0, HEADS, 4, head_scores)

    for index in range(max(len(steps) - 1, levels - 1)):
        if index + 1 < len(steps):
            steps[index + 1]()
        if index < levels - 1:
            gather_level(index)

    def head_attended(h):
        at = head_columns(h)
        attended = contract(scores[h], value_ref[:, at], 1, 0)
        attended = attended + contract(query_ref[:, at], prefix[at, :], 1, 0)
        turned = attended.T.astype(jnp.bfloat16)
        pieces = HEAD // shard_rows

        def put():
            for piece in range(pieces):
                shard = h * pieces + piece
                top = pl.multiple_of(shard // 2 * shard_rows, shard_rows)
                att[shard % 2, pl.ds(top, shard_rows), :] = turned[
                    piece * shard_rows : (piece + 1) * shard_rows, :
                ]

        return put

    each_head(0, HEADS, 4, head_attended)

    att_swap = swap(att.at[1 - core], sib_att, 1)
    att_swap.start()
    grad_swap.wait()
    att_swap.wait()
    height = group * shard_rows
    for first in range(0, seq_count // 2, group):
        strip = pl.ds(first * shard_rows, height)
        for d in range(data_count):
            across = slice(d * columns, (d + 1) * columns)
            panel = contract(att[core, strip, :], grad_ref[:, across], 1, 0)
            panel = panel + contract(sib_att[strip, :], sib_grad[:, across], 1, 0)
            panel = (grad_scale * panel).astype(jnp.bfloat16)
            for g in range(group):
                for s in range(STREAMS):
                    top = (g * STREAMS + s) * rows
                    sums[s, place(orders[s], 2 * (first + g), d)] = panel[top : top + rows, :]
    for s in range(STREAMS):
        reduce_hop(s, levels - 1).start()

    gather_level(levels - 1)
    half = away.shape[1]
    for first in range(0, seq_count // 2, group):
        panel = jnp.concatenate(
            [
                jnp.concatenate(
                    [held[s, place(orders[s], 2 * j, d)] for d in range(data_count)], axis=1
                )
                for j in range(first, first + group)
                for s in range(STREAMS)
            ],
            axis=0,
        )
        strip = slice(first * shard_rows, first * shard_rows + height)
        away[:, strip] = contract(sib_grad[...], panel, 1, 1).astype(jnp.bfloat16)
        mine = contract(grad_ref[...], panel, 1, 1).astype(jnp.bfloat16)
        for side in range(2):

            @pl.when(core == side)
            def _():
                for g in range(group):
                    left = (2 * (first + g) + side) * shard_rows
                    head_grad[:, left : left + shard_rows] = mine[
                        :, g * shard_rows : (g + 1) * shard_rows
                    ]

    back = swap(away, landed, 2)
    back.start()
    back.wait()
    for side in range(2):

        @pl.when(core != side)
        def _():
            for j in range(seq_count // 2):
                left = (2 * j + side) * shard_rows
                head_grad[:, left : left + shard_rows] = landed[
                    :, j * shard_rows : (j + 1) * shard_rows
                ]

    def query_dout(h):
        at = head_columns(h)
        product = contract(query_ref[:, at], head_grad[:, at], 0, 0)
        return functools.partial(store, part, (at, slice(None)), product)

    each_head(0, HEADS, 4, query_dout)

    steps = sum_steps(
        part, suffix, score_scale, True,
        tuple(ref.at[1] for ref in scan + (scan_send, scan_recv)), seq_count,
    )
    steps[0]()

    def local_head(h):
        at = head_columns(h)
        rows_g, rows_q, rows_k = head_grad[:, at], query_ref[:, at], key_ref[:, at]
        grad_scores = (
            score_scale * contract(rows_g, value_ref[:, at], 1, 1) * causal
        ).astype(jnp.bfloat16)
        queried = contract(grad_scores, rows_k, 1, 0) + contract(rows_g, prefix[at, :], 1, 1)
        keyed = contract(grad_scores, rows_q, 0, 0)
        valued = contract(scores[h], rows_g, 0, 0)

        def put():
            query_out[:, at] = queried.astype(jnp.bfloat16)
            key_sum[:, at] = keyed
            value_sum[:, at] = valued

        return put

    chunks = len(steps) - 1
    for index in range(max(chunks, levels - 1)):
        if index < chunks:
            each_head(HEADS * index // chunks, HEADS * (index + 1) // chunks, 4, local_head)
            steps[index + 1]()
        if index < levels - 1:
            reduce_level(levels - 1 - index)

    def last_terms(h):
        at = head_columns(h)
        keyed = key_sum[:, at] + contract(value_ref[:, at], suffix[at, :], 1, 1)
        valued = value_sum[:, at] + contract(key_ref[:, at], suffix[at, :], 1, 0)

        def put():
            key_out[:, at] = keyed.astype(jnp.bfloat16)
            value_out[:, at] = valued.astype(jnp.bfloat16)

        return put

    each_head(0, HEADS, 4, last_terms)

    reduce_level(0)


def shards(queries, key_rows, value_rows, out_grad, out_weight):
    tokens = queries.shape[1]
    seq_count = lax.axis_size("seq")
    data_count = lax.axis_size("dp")
    seq_length = tokens * seq_count
    score_scale = 1.0 / math.sqrt(HEAD * seq_length)
    grad_scale = 1.0 / math.sqrt(queries.shape[0] * data_count * seq_length)
    features = queries.shape[2]
    shard_rows, columns = out_weight.shape
    width = out_grad.shape[2]
    hops = log2(seq_count // 2)
    levels = hops + log2(data_count)
    bf16, f32 = jnp.bfloat16, jnp.float32
    blocks = (STREAMS, 2**levels, shard_rows // STREAMS, columns)
    half = features // 2
    vmem = pl.BlockSpec(memory_space=pltpu.VMEM)
    dma = pltpu.SemaphoreType.DMA
    flat = jax.ShapeDtypeStruct((tokens, features), bf16)
    query_grad, key_grad, value_grad, weight_grad = pl.pallas_call(
        functools.partial(kernel, seq_count, data_count, score_scale, grad_scale),
        out_shape=(flat, flat, flat, jax.ShapeDtypeStruct((shard_rows, columns), f32)),
        in_specs=[vmem] * 5,
        out_specs=(vmem,) * 4,
        scratch_shapes=[
            pltpu.VMEM(blocks, bf16),
            pltpu.VMEM(blocks, bf16),
            pltpu.VMEM(blocks, bf16),
            pltpu.VMEM((tokens, width), bf16),
            pltpu.VMEM((tokens, features), bf16),
            pltpu.VMEM((tokens, half), bf16),
            pltpu.VMEM((tokens, half), bf16),
            pltpu.VMEM((2, half, tokens), bf16),
            pltpu.VMEM((half, tokens), bf16),
            pltpu.VMEM((HEADS, tokens, tokens), bf16),
            pltpu.VMEM((tokens, features), f32),
            pltpu.VMEM((tokens, features), f32),
            pltpu.VMEM((features, HEAD), f32),
            pltpu.VMEM((features, HEAD), bf16),
            pltpu.VMEM((features, HEAD), bf16),
            pltpu.VMEM((2, features, HEAD), bf16),
            pltpu.VMEM((2, features, HEAD), bf16),
            pltpu.VMEM((2, half, HEAD), f32),
            pltpu.VMEM((2, half, HEAD), f32),
            pltpu.VMEM((2, hops + 1, half, HEAD), bf16),
            pltpu.VMEM((2, hops + 1, half, HEAD), bf16),
            dma((STREAMS, levels)),
            dma((STREAMS, levels)),
            dma((STREAMS, levels)),
            dma((STREAMS, levels)),
            dma((3,)),
            dma((3,)),
            dma((2, hops + 2)),
            dma((2, hops + 2)),
        ],
        compiler_params=pltpu.CompilerParams(
            collective_id=0, has_side_effects=True, vmem_limit_bytes=56 << 20
        ),
    )(queries[0], key_rows[0], value_rows[0], out_grad[0], out_weight)
    return query_grad[None], key_grad[None], value_grad[None], weight_grad


def solution(mesh):
    return jax.shard_map(
        shards,
        mesh=mesh,
        in_specs=(
            P("dp", "seq", None),
            P("dp", "seq", None),
            P("dp", "seq", None),
            P("dp", "seq", None),
            P("seq", "dp"),
        ),
        out_specs=(
            P("dp", "seq", None),
            P("dp", "seq", None),
            P("dp", "seq", None),
            P("seq", "dp"),
        ),
        check_vma=False,
    )
```
